32 devices in a mesh: grp: 2 (over x), row: 4 (over z), col: 4 (over y, core).
Axes of the slice: x: 2, y: 2, z: 4, core: 2. Of those that a mesh axis runs over, the one named last changes fastest.
Arguments:
- activations: bfloat16 [128, 64, 8192], P(('grp', 'col'), None, 'row'), may hold values from -6 to 6
- out_grads: bfloat16 [128, 64, 8192], P(('grp', 'col'), None, 'row'), may hold values from -6 to 6
- proj_in: bfloat16 [8192, 128], P('row'), may hold values from -0.0625 to 0.0625
- proj_out: bfloat16 [8192, 128], P('row'), may hold values from -0.0625 to 0.0625
- fisher_inv: float32 [16384, 16384], P('row', ('grp', 'col')), may hold values from -1 to 4, as said below
- store: bfloat16 [16384, 16384], P('row', ('grp', 'col')), may hold values from -0.046875 to 0.046875
- lengths: int32 [128], P(('grp', 'col')), may hold values from 1 to 64, as said below
- judge_ids: int32 [128], replicated, may hold values from 0 to 63, as said below
Outputs:
- node_scores: float32 [16384, 64], P('row')
The draws below stay inside these ranges and needn't reach their ends.
Inputs may be any that keep to these rules, and one draw needn't show every extreme that they name: lengths[b] is how many of branch b's first token slots count; the rest are padding. `judge_ids`: every node id names at least one branch. fisher_inv is symmetric.
All inputs are finite; a program needn't handle non-finite values.
Results may differ from the reference program's by a relative error of at most 0.0029.
Values may be sent and summed in bfloat16 or wider, within the bound.
No kernel may reach another device: no remote copies, remote signals or barrier semaphores. Data moves between devices by JAX's collectives and lax.ppermute only.
A program may use at most 128 MiB of HBM per device.

```python
import math
import jax
import jax.numpy as jnp
from jax import lax

D = 8192
RANK = 128
L = 64
FEATS = 16384
BRANCHES = 128
STORE = 16384
NODES = 64


def draw_fisher_inv(key, part):
    key_off = jax.random.fold_in(key, 11)
    key_diag = jax.random.fold_in(key, 12)
    spread = 0.5
    diag_vals = jnp.exp(jax.random.uniform(key_diag, (FEATS,), jnp.float32, jnp.log(0.5), jnp.log(2.0)))
    base = jnp.clip(jax.random.normal(key_off, (FEATS, FEATS), jnp.float32), -6.0, 6.0) * (spread / jnp.sqrt(FEATS * 1.0))
    symmetric = base + base.T
    return symmetric + jnp.diag(diag_vals)


def draw_lengths(key, part):
    key_len = jax.random.fold_in(key, 21)
    key_pick = jax.random.fold_in(key, 22)
    drawn = jax.random.randint(key_len, (BRANCHES,), 1, L + 1)
    picked = jax.random.randint(key_pick, (), 0, BRANCHES)
    return jnp.where(jnp.arange(BRANCHES) == picked, L, drawn).astype(jnp.int32)


def draw_judge_ids(key, part):
    key_first = jax.random.fold_in(key, 31)
    key_rest = jax.random.fold_in(key, 32)
    key_order = jax.random.fold_in(key, 33)
    first = jax.random.permutation(key_first, NODES)
    rest = jax.random.randint(key_rest, (BRANCHES - NODES,), 0, NODES)
    joined = jnp.concatenate([first.astype(jnp.int32), rest.astype(jnp.int32)])
    return jax.random.permutation(key_order, joined).astype(jnp.int32)


def shard_levels(key, shape, cuts, smallest, largest):
    level = 1.0
    for position, blocks in cuts:
        steps = jax.random.uniform(jax.random.fold_in(jax.random.fold_in(key, 6), position), (blocks,), jnp.float32, smallest / len(cuts), largest / len(cuts))
        level = level * jnp.repeat(jnp.exp(steps), shape[position] // blocks).reshape((-1,) + (1,) * (len(shape) - 1 - position))
    return level


def gaussian(stream_key, shape, deviation, reach, cuts=(), held_as=jnp.bfloat16):
    array = jax.random.normal(stream_key, shape, jnp.float32) * deviation
    if len(cuts) > 0:
        array = shard_levels(stream_key, shape, cuts, -0.22, 0.18) * array
    return jnp.clip(array, min=-reach, max=reach).astype(held_as)


def setup_inputs(seed: int = 0) -> dict:
    keys = jax.random.split(jax.random.key(seed), 9)
    activations = gaussian(keys[0], (BRANCHES, L, D), 1.0, 6.0, ((0, 8), (2, 4)))
    out_grads = gaussian(keys[1], (BRANCHES, L, D), 1.0, 6.0, ((0, 8), (2, 4)))
    proj_in = gaussian(keys[2], (D, RANK), D ** -0.5, 0.0625, ((0, 4),))
    proj_out = gaussian(keys[3], (D, RANK), D ** -0.5, 0.0625, ((0, 4),))
    fisher_inv = draw_fisher_inv(jax.random.fold_in(keys[8], 71), 0)
    store = gaussian(keys[5], (STORE, FEATS), FEATS ** -0.5, 0.046875, ((0, 4), (1, 8)))
    lengths = draw_lengths(jax.random.fold_in(keys[8], 71), 0)
    judge_ids = draw_judge_ids(jax.random.fold_in(keys[8], 71), 0)
    return {"activations": activations, "out_grads": out_grads, "proj_in": proj_in, "proj_out": proj_out, "fisher_inv": fisher_inv, "store": store, "lengths": lengths, "judge_ids": judge_ids}


def reference(activations, out_grads, proj_in, proj_out, fisher_inv, store, lengths, judge_ids):
    high = lax.Precision.HIGHEST
    flat_act = activations.reshape(BRANCHES * L, D).astype(jnp.float32)
    flat_grad = out_grads.reshape(BRANCHES * L, D).astype(jnp.float32)
    act_proj = jnp.dot(flat_act, proj_in.astype(jnp.float32), precision=high).reshape(BRANCHES, L, RANK)
    grad_proj = jnp.dot(flat_grad, proj_out.astype(jnp.float32), precision=high).reshape(BRANCHES, L, RANK)
    token_mask = (jnp.arange(L)[None, :] < lengths[:, None]).astype(jnp.float32)
    weighted = grad_proj * token_mask[:, :, None]
    grads = jnp.einsum('bto,bti->boi', weighted, act_proj, precision=high) * (1.0 / math.sqrt(L))
    grads = grads.reshape(BRANCHES, FEATS)
    pre = lax.dot_general(fisher_inv, grads, (((1,), (1,)), ((), ())), precision=high)
    pre_half = pre.astype(jnp.bfloat16)
    scores = jnp.dot(store.astype(jnp.float32), pre_half.astype(jnp.float32), precision=high)
    onehot = (judge_ids[:, None] == jnp.arange(NODES)[None, :]).astype(jnp.float32)
    return jnp.dot(scores, onehot, precision=high)
```

```python
import functools
import math

import jax
import jax.numpy as jnp
from jax import lax
from jax.experimental import pallas as pl
from jax.experimental.pallas import tpu as pltpu
from jax.sharding import PartitionSpec as P


LANES = 128
TAIL = 16
TOP = 32700.0
STEP = 128.0
TINY = 1e-37
F32 = jnp.float32
BF16 = jnp.bfloat16
I16 = jnp.int16
I32 = jnp.int32

VMEM_SPEC = pl.BlockSpec(memory_space=pltpu.VMEM)
SMEM_SPEC = pl.BlockSpec(memory_space=pltpu.SMEM)
HBM_SPEC = pl.BlockSpec(memory_space=pltpu.HBM)


def in_hbm(value):
    return pltpu.with_memory_space_constraint(value, pltpu.HBM)


def params(mib):
    return pltpu.CompilerParams(vmem_limit_bytes=mib << 20)


def diagonal(rows):
    down = lax.broadcasted_iota(I32, (rows, LANES), 0)
    across = lax.broadcasted_iota(I32, (rows, LANES), 1)
    return down == across


def encode(x):
    peak = jnp.maximum(jnp.max(jnp.abs(x), axis=1, keepdims=True), TINY)
    code = jnp.ceil(jnp.log2(peak) * STEP)
    scaled = x * jnp.exp2(code * (-1.0 / STEP)) * TOP
    values = jnp.clip(jnp.round(scaled), -32767.0, 32767.0)
    across = jnp.sum(jnp.where(diagonal(x.shape[0]), code, 0.0), axis=0, keepdims=True)
    return values.astype(I32).astype(I16), across


def decode(values, across):
    rows = values.shape[0]
    code = jnp.sum(jnp.where(diagonal(rows), across, 0.0), axis=1, keepdims=True)
    return values.astype(I32).astype(F32) * (jnp.exp2(code * (1.0 / STEP)) * (1.0 / TOP))


def put_tail(rows_of_codes):
    down = lax.broadcasted_iota(I32, (TAIL, LANES), 0)
    tile = jnp.zeros((TAIL, LANES), F32)
    for index, codes in enumerate(rows_of_codes):
        tile = jnp.where(down == index, codes, tile)
    return tile.astype(I32).astype(I16)


def get_tail(tile):
    return tile.astype(I32).astype(F32)


def write_message(ref, x, start=0):
    rows = x.shape[0]
    values, codes = encode(x)
    ref[pl.ds(start, rows), :] = values
    ref[pl.ds(start + rows, TAIL), pl.ds(0, LANES)] = put_tail([codes])


def read_message(ref, rows, start=0):
    tail = get_tail(ref[pl.ds(start + rows, TAIL), pl.ds(0, LANES)])
    return decode(ref[pl.ds(start, rows), :], tail[0:1, :])


def write_blocks(ref, blocks):
    rows = blocks[0].shape[0]
    tails = []
    for index, x in enumerate(blocks):
        peak = jnp.max(jnp.max(jnp.abs(x), axis=0, keepdims=True), axis=1, keepdims=True)
        code = jnp.ceil(jnp.log2(jnp.maximum(peak, TINY)) * STEP)
        scaled = x * jnp.exp2(code * (-1.0 / STEP)) * TOP
        values = jnp.clip(jnp.round(scaled), -32767.0, 32767.0)
        ref[index * rows : (index + 1) * rows, :] = values.astype(I32).astype(I16)
        tails.append(jnp.broadcast_to(code, (1, LANES)))
    ref[len(blocks) * rows :, :] = put_tail(tails)


def position():
    column = lax.axis_index("col")
    return lax.axis_index("row"), lax.axis_index("grp"), column // 2, lax.rem(column, 2)


def project_kernel(shift, ring, first, act, grad, w_act, w_grad, out, *refs):
    tokens, width = refs[-3].shape
    rank = w_act.shape[1]
    act_here, grad_here, sems = refs[-3:]
    start = pl.multiple_of(lax.rem(lax.axis_index("row") + shift, ring) * tokens, tokens)
    moves = [(act.at[pl.ds(start, tokens), :], act_here), (grad.at[pl.ds(start, tokens), :], grad_here)]
    weights = (w_act, w_grad)
    if first:
        weights = refs[:2]
        moves = [(w_act, weights[0]), moves[0], (w_grad, weights[1]), moves[1]]
    copies = [pltpu.make_async_copy(*move, sems.at[i]) for i, move in enumerate(moves)]
    for copy in copies:
        copy.start()
    each = len(copies) // 2
    for half, here in enumerate((act_here, grad_here)):
        for copy in copies[half * each : (half + 1) * each]:
            copy.wait()
        columns = slice(half * rank, (half + 1) * rank)
        total = jnp.dot(here[...], weights[half][...], preferred_element_type=F32)
        if shift == 0:
            out[:, columns] = total
            continue
        tails = []
        for begin in range(0, tokens, LANES):
            stop = min(begin + LANES, tokens)
            values, codes = encode(total[begin:stop])
            out[begin:stop, columns] = values
            tails.append(codes)
        out[tokens:, columns] = put_tail(tails)


def project(act, grad, w_act, w_grad, tokens, shift, ring, first):
    width, rank = w_act.shape
    coded = shift != 0
    shape = (tokens + TAIL, 2 * rank) if coded else (tokens, 2 * rank)
    out_shape = [jax.ShapeDtypeStruct(shape, I16 if coded else F32)]
    if first:
        out_shape += [pltpu.VMEM((width, rank), BF16)] * 2
    weight_spec = HBM_SPEC if first else VMEM_SPEC
    return pl.pallas_call(
        functools.partial(project_kernel, shift, ring, first),
        out_shape=out_shape,
        in_specs=[HBM_SPEC, HBM_SPEC, weight_spec, weight_spec],
        out_specs=[VMEM_SPEC] * len(out_shape),
        scratch_shapes=[
            pltpu.VMEM((tokens, width), BF16),
            pltpu.VMEM((tokens, width), BF16),
            pltpu.SemaphoreType.DMA((4,)),
        ],
        compiler_params=params(5),
        name=f"project{shift}",
    )(act, grad, w_act, w_grad)


def outer_kernel(ring, slots, lengths, own, *refs):
    row = lax.axis_index("row")
    received, outs, total, whole = refs[: ring - 1], refs[ring - 1 : -2], refs[-2], refs[-1]
    tokens = own.shape[0]
    rank = own.shape[1] // 2
    quarter = tokens // slots
    for half in range(2):
        columns = slice(half * rank, (half + 1) * rank)
        tails = [get_tail(ref[tokens:, columns]) for ref in received]
        for index, start in enumerate(range(0, tokens, LANES)):
            stop = min(start + LANES, tokens)
            value = own[start:stop, columns]
            for ref, tail in zip(received, tails):
                value += decode(ref[start:stop, columns], tail[index : index + 1, :])
            total[start:stop, columns] = value
    for j in range(quarter):
        rows = slice(j * slots, (j + 1) * slots)
        token = lax.broadcasted_iota(I32, (slots, rank), 0)
        kept = token < lengths[row * quarter + j]
        weighted = jnp.where(kept, total[rows, rank:], 0.0)
        whole[j] = lax.dot_general(
            weighted,
            total[rows, :rank],
            (((0,), (0,)), ((), ())),
            precision=lax.Precision.HIGHEST,
            preferred_element_type=F32,
        ) * (1.0 / math.sqrt(slots))
    span = rank // ring
    for shift in range(ring):
        first = pl.multiple_of(lax.rem(row + shift, ring) * span, span)
        write_blocks(outs[shift], [whole[j, pl.ds(first, span), :] for j in range(quarter)])


def outer(lengths, own, received, ring, slots):
    tokens = own.shape[0]
    rank = own.shape[1] // 2
    quarter = tokens // slots
    rows = quarter * rank // ring
    return pl.pallas_call(
        functools.partial(outer_kernel, ring, slots),
        out_shape=[jax.ShapeDtypeStruct((rows + TAIL, rank), I16)] * ring,
        in_specs=[SMEM_SPEC] + [VMEM_SPEC] * ring,
        out_specs=[VMEM_SPEC] * ring,
        scratch_shapes=[pltpu.VMEM((tokens, 2 * rank), F32), pltpu.VMEM((quarter, rank, rank), F32)],
        compiler_params=params(4),
        name="outer",
    )(lengths, own, *received)


def source(shift, sizes, other):
    _, group, pair, core = position()
    group = lax.rem(group - shift[0] + sizes[0], sizes[0])
    pair = lax.rem(pair - shift[1] + sizes[1], sizes[1])
    return group, pair, 1 - core if other else core


def gather_kernel(ring, sizes, shifts, quarter, judge, *refs):
    messages, out, total = refs[:-2], refs[-2], refs[-1]
    nodes, span, rank = total.shape
    rows = quarter * span
    row = lax.axis_index("row")
    total[...] = jnp.zeros_like(total)
    for index, ref in enumerate(messages):
        other, which = divmod(index, len(shifts))
        group, pair, core = source(shifts[which], sizes, other)
        block = (group * sizes[1] + pair) * 2 + core
        for shift in range(ring):
            start = shift * (rows + TAIL)
            tail = get_tail(ref[start + rows : start + rows + TAIL, :])
            scale = jnp.exp2(tail * (1.0 / STEP)) * (1.0 / TOP)
            first = (block * ring + lax.rem(row - shift + ring, ring)) * quarter
            for j in range(quarter):
                node = judge[first + j]
                value = ref[start + j * span : start + (j + 1) * span, :].astype(I32).astype(F32)
                total[node] = total[node] + value * scale[j : j + 1, :]
    for o in range(span):
        value = total[:, o, :]
        high = value.astype(BF16)
        out[:nodes, o * rank : (o + 1) * rank] = high
        out[nodes:, o * rank : (o + 1) * rank] = (value - high.astype(F32)).astype(BF16)


def gather(judge, messages, ring, sizes, shifts, quarter, nodes, rank):
    span = rank // ring
    return pl.pallas_call(
        functools.partial(gather_kernel, ring, sizes, shifts, quarter),
        out_shape=jax.ShapeDtypeStruct((2 * nodes, span * rank), BF16),
        in_specs=[SMEM_SPEC] + [VMEM_SPEC] * len(messages),
        out_specs=VMEM_SPEC,
        scratch_shapes=[pltpu.VMEM((nodes, span, rank), F32)],
        compiler_params=params(4),
        name="gather",
    )(judge, *messages)


def fisher_fetch_kernel(shift, ring, fisher_inv, high_out, low_out, held, sems):
    rows, width = held.shape
    count = sems.shape[0]
    block = rows // count
    start = pl.multiple_of(lax.rem(lax.axis_index("row") + shift, ring) * width, width)
    copies = []
    for i in range(count):
        here = pl.ds(i * block, block)
        copies.append(
            pltpu.make_async_copy(fisher_inv.at[here, pl.ds(start, width)], held.at[here, :], sems.at[i])
        )
    for copy in copies:
        copy.start()
    for i, copy in enumerate(copies):
        copy.wait()
        here = slice(i * block, (i + 1) * block)
        value = held[here, :]
        high = value.astype(BF16)
        high_out[here, :] = high
        low_out[here, :] = (value - high.astype(F32)).astype(BF16)


def fisher_fetch(fisher_inv, shift, ring):
    rows, columns = fisher_inv.shape
    width = columns // ring
    return pl.pallas_call(
        functools.partial(fisher_fetch_kernel, shift, ring),
        out_shape=[pltpu.VMEM((rows, width), BF16)] * 2,
        in_specs=[HBM_SPEC],
        out_specs=[VMEM_SPEC] * 2,
        scratch_shapes=[pltpu.VMEM((rows, width), F32), pltpu.SemaphoreType.DMA((8,))],
        compiler_params=params(10),
        name=f"fisher_fetch{shift}",
    )(fisher_inv)


def fisher_kernel(coded, left, high, low, out):
    nodes = left.shape[0] // 2
    both = jnp.dot(left[...], high[...], preferred_element_type=F32)
    rest = jnp.dot(left[:nodes, :], low[...], preferred_element_type=F32)
    total = both[:nodes, :] + (both[nodes:, :] + rest)
    if coded:
        write_message(out, total)
    else:
        out[...] = total


def fisher_part(left, high, low, shift):
    nodes = left.shape[0] // 2
    width = high.shape[1]
    coded = shift != 0
    return pl.pallas_call(
        functools.partial(fisher_kernel, coded),
        out_shape=jax.ShapeDtypeStruct((nodes + TAIL if coded else nodes, width), I16 if coded else F32),
        in_specs=[VMEM_SPEC] * 3,
        out_specs=VMEM_SPEC,
        compiler_params=params(4),
        name=f"fisher{shift}",
    )(left, high, low)


def add_kernel(own, *refs):
    received, out = refs[:-1], refs[-1]
    rows = own.shape[0]
    total = own[...]
    for ref in received:
        total += read_message(ref, rows)
    write_message(out, total)


def add_parts(own, received, name):
    rows, columns = own.shape
    return pl.pallas_call(
        add_kernel,
        out_shape=jax.ShapeDtypeStruct((rows + TAIL, columns), I16),
        in_specs=[VMEM_SPEC] * (1 + len(received)),
        out_specs=VMEM_SPEC,
        compiler_params=params(4),
        name=name,
    )(own, *received)


def store_fetch_kernel(shift, ring, store, out, sems):
    rows, width = out.shape
    count = sems.shape[0]
    block = rows // count
    chunk = lax.rem(lax.axis_index("row") - shift + ring, ring)
    start = pl.multiple_of(chunk * width, width)
    copies = []
    for i in range(count):
        here = pl.ds(i * block, block)
        copies.append(pltpu.make_async_copy(store.at[here, pl.ds(start, width)], out.at[here, :], sems.at[i]))
    for copy in copies:
        copy.start()
    for copy in copies:
        copy.wait()


def store_fetch(store, shift, ring):
    rows, columns = store.shape
    return pl.pallas_call(
        functools.partial(store_fetch_kernel, shift, ring),
        out_shape=pltpu.VMEM((rows, columns // ring), BF16),
        in_specs=[HBM_SPEC],
        out_specs=VMEM_SPEC,
        scratch_shapes=[pltpu.SemaphoreType.DMA((4,))],
        compiler_params=params(1),
        name=f"store_fetch{shift}",
    )(store)


def score_kernel(count, last, *refs):
    messages, stores, refs = refs[:count], refs[count : 2 * count], refs[2 * count :]
    nodes = messages[0].shape[0] - TAIL
    rows = stores[0].shape[0]
    pieces = []
    for message in messages:
        value = read_message(message, nodes)
        high = value.astype(BF16)
        pieces.append(jnp.concatenate([high, (value - high.astype(F32)).astype(BF16)], axis=0))
    core = position()[3]
    steps = 4
    block = rows // steps
    for step in range(steps):
        here = pl.ds(pl.multiple_of(lax.rem(step + (1 - core) * (steps // 2), steps) * block, block), block)
        total = 0.0
        if last:
            total = refs[0][:, here]
        for piece, store in zip(pieces, stores):
            both = lax.dot_general(
                piece, store[here, :], (((1,), (1,)), ((), ())), preferred_element_type=F32
            )
            total += both[:nodes, :] + both[nodes:, :]
        if last:
            out = refs[1 + step // (steps // 2)]
            offset = step % (steps // 2) * block
            out[:, offset : offset + block] = total
        else:
            refs[0][:, here] = total


def score(messages, stores, before, name):
    nodes = messages[0].shape[0] - TAIL
    rows = stores[0].shape[0]
    last = before is not None
    operands = list(messages) + list(stores) + ([before] if last else [])
    half = jax.ShapeDtypeStruct((nodes, rows // 2), F32)
    return pl.pallas_call(
        functools.partial(score_kernel, len(messages), last),
        out_shape=[half, half] if last else jax.ShapeDtypeStruct((nodes, rows), F32),
        in_specs=[VMEM_SPEC] * len(operands),
        out_specs=[VMEM_SPEC, VMEM_SPEC] if last else VMEM_SPEC,
        compiler_params=params(6),
        name=name,
    )(*operands)


def split_kernel(sizes, shifts, mine, theirs, own, *outs):
    groups, pairs = sizes
    _, group_here, pair_here, _ = position()
    width = own.shape[1]
    for shift, out in zip(shifts, (own,) + outs):
        group = lax.rem(group_here + shift[0], groups)
        pair = lax.rem(pair_here + shift[1], pairs)
        first = pl.multiple_of((group * pairs + pair) * width, width)
        value = mine[:, pl.ds(first, width)] + theirs[:, pl.ds(first, width)]
        if out is own:
            out[...] = value
        else:
            write_message(out, value)


def split(mine, theirs, sizes, shifts):
    nodes, columns = mine.shape
    width = columns // len(shifts)
    return pl.pallas_call(
        functools.partial(split_kernel, sizes, shifts),
        out_shape=[jax.ShapeDtypeStruct((nodes, width), F32)]
        + [jax.ShapeDtypeStruct((nodes + TAIL, width), I16)] * (len(shifts) - 1),
        in_specs=[VMEM_SPEC, VMEM_SPEC],
        out_specs=[VMEM_SPEC] * len(shifts),
        compiler_params=params(4),
        name="split",
    )(mine, theirs)


def join_kernel(sizes, shifts, *refs):
    messages, out = refs[:-1], refs[-1]
    nodes = out.shape[0]
    width = messages[0].shape[1]
    for index, ref in enumerate(messages):
        other, which = divmod(index, len(shifts))
        group, pair, core = source(shifts[which], sizes, other)
        spot = core * len(shifts) + group * sizes[1] + pair
        out[:, pl.ds(pl.multiple_of(spot * width, width), width)] = read_message(ref, nodes)


def join(messages, sizes, shifts):
    nodes = messages[0].shape[0] - TAIL
    width = messages[0].shape[1]
    return pl.pallas_call(
        functools.partial(join_kernel, sizes, shifts),
        out_shape=jax.ShapeDtypeStruct((nodes, width * len(messages)), F32),
        in_specs=[VMEM_SPEC] * len(messages),
        out_specs=VMEM_SPEC,
        compiler_params=params(4),
        name="join",
    )(*messages)


def local(sizes, ring, activations, out_grads, proj_in, proj_out, fisher_inv, store, lengths, judge_ids):
    br_here, slots, width = activations.shape
    rank = proj_in.shape[1]
    groups, pairs = sizes
    nodes = judge_ids.shape[0] // 2
    quarter = br_here // ring
    tokens = quarter * slots
    shifts = tuple((g, p) for g in range(groups) for p in range(pairs))

    def along(value, shift):
        return lax.ppermute(value, "row", [(i, (i + shift) % ring) for i in range(ring)])

    def across(value, shift):
        pairs_of = []
        for g in range(groups):
            for p in range(pairs):
                for core in range(2):
                    to = ((g + shift[0]) % groups * pairs + (p + shift[1]) % pairs) * 2 + core
                    pairs_of.append(((g * pairs + p) * 2 + core, to))
        return lax.ppermute(value, ("grp", "col"), pairs_of)

    def swap(value):
        return lax.ppermute(value, "col", [(i, i ^ 1) for i in range(2 * pairs)])

    order = sorted(range(1, ring), key=lambda shift: -min(shift, ring - shift))

    flat_act = in_hbm(activations.reshape(br_here * slots, width))
    flat_grad = in_hbm(out_grads.reshape(br_here * slots, width))
    weights = in_hbm(proj_in), in_hbm(proj_out)
    fisher_inv, store = in_hbm(fisher_inv), in_hbm(store)
    parts = {}
    for shift in order + [0]:
        first = len(parts) == 0
        parts[shift], *held = project(flat_act, flat_grad, *weights, tokens, shift, ring, first)
        weights = held if first else weights
    received = [along(parts[shift], shift) for shift in order]
    blocks = outer(lengths, parts[0], received, ring, slots)
    blocks = [blocks[0]] + [along(blocks[shift], shift) for shift in range(1, ring)]
    mine = jnp.concatenate(blocks, axis=0)
    near = [mine] + [across(mine, shift) for shift in shifts[1:]]
    far = [swap(message) for message in near]
    left = gather(judge_ids, near + far, ring, sizes, shifts, quarter, nodes, rank)

    fetched = {shift: fisher_fetch(fisher_inv, shift, ring) for shift in order + [0]}
    parts = {shift: fisher_part(left, *fetched[shift], shift) for shift in order + [0]}
    received = [along(parts[shift], shift) for shift in order]
    stores = [store_fetch(store, shift, ring) for shift in range(ring)]
    pre = add_parts(parts[0], received, "sum_pre")
    scores = score([pre], stores[:1], None, "score_own")
    others = [along(pre, shift) for shift in range(1, ring)]
    sent, kept = score(others, stores[1:], scores, "score_rest")
    parts = split(kept, swap(sent), sizes, shifts)
    received = [across(part, shift) for part, shift in zip(parts[1:], shifts[1:])]
    final = add_parts(parts[0], received, "sum_scores")
    near = [final] + [across(final, shift) for shift in shifts[1:]]
    far = [swap(message) for message in near]
    return join(near + far, sizes, shifts).T


def solution(mesh):
    placed = (
        P(("grp", "col"), None, "row"),
        P(("grp", "col"), None, "row"),
        P("row", None),
        P("row", None),
        P("row", ("grp", "col")),
        P("row", ("grp", "col")),
        P(("grp", "col")),
        P(),
    )
    sizes = (mesh.shape["grp"], mesh.shape["col"] // 2)
    return jax.shard_map(
        functools.partial(local, sizes, mesh.shape["row"]),
        mesh=mesh,
        in_specs=placed,
        out_specs=P("row", None),
        check_vma=False,
    )
```
